32 devices in a mesh: pb: 4 (over x, core), ka: 4 (over z), ga: 2 (over y).
Axes of the slice: x: 2, y: 2, z: 4, core: 2. Of those that a mesh axis runs over, the one named last changes fastest.
Arguments:
- queries: bfloat16 [16, 512, 768], P(None, 'pb', 'ga'), may hold values from -6 to 6
- comp_keys: bfloat16 [1024, 768], P(('ka', 'pb'), 'ga'), may hold values from -6 to 6
- comp_values: bfloat16 [1024, 512], P(('ka', 'pb'), 'ga'), may hold values from -6 to 6
- outputs: bfloat16 [16, 512, 512], P(None, 'pb', 'ga'), may hold values from -1.1953125 to 1.1953125
- grad_out: bfloat16 [16, 512, 512], P(None, 'pb', 'ga'), may hold values from -300 to 300
- log_sums: float32 [4, 16, 512], P('ga', None, 'pb'), may hold values from 7 to 10
- visible: int32 [8, 1024], P('pb', 'ka'), may hold values from 0 to 1, as said below
Outputs:
- grad_queries: float32 [16, 512, 768], P('ka', 'pb', 'ga')
- grad_keys: float32 [1024, 768], P(('ka', 'pb'), 'ga')
- grad_values: float32 [1024, 512], P(('ka', 'pb'), 'ga')
The draws below stay inside these ranges and needn't reach their ends.
Inputs may be any that keep to these rules, and one draw needn't show every extreme that they name: The queries are the last 512 positions of a sequence of 16384 positions, and compressed key j covers positions 16 * j to 16 * j + 31. visible[b, j] is 1 exactly when key j ends before the first position of query block b and starts no earlier than the start of the document that holds that position; the sequence is packed from a few documents.
All inputs are finite; a program needn't handle non-finite values.
Results may differ from the reference program's by a relative error of at most 0.0029.
Values may be sent and summed in bfloat16 or wider, within the bound.
A program may use at most 64 MiB of HBM per device.

```python
import math
import jax
import jax.numpy as jnp
from jax import lax

G = 4
HG = 16
DK = 192
DV = 128
QBLK = 64
STRIDE = 16
SPAN = 32
NQ = 512
KEYS = 1024
NQB = 8


def draw_visible(key, part):
    positions = KEYS * STRIDE
    starts = jax.random.randint(jax.random.fold_in(key, 11), (2,), 0, positions)
    window_start = positions - NQB * QBLK
    block_first = window_start + jnp.arange(NQB, dtype=jnp.int32) * QBLK
    key_first = jnp.arange(KEYS, dtype=jnp.int32) * STRIDE
    key_last = key_first + SPAN - 1
    doc_start = jnp.max(jnp.where(starts[None, :] <= block_first[:, None], starts[None, :], 0), axis=1)
    drawn = (key_last[None, :] < block_first[:, None]) & (key_first[None, :] >= doc_start[:, None])
    return drawn.astype(jnp.int32)


def block_scale(key, dims, pieces, smallest, high):
    def one(dim, blocks):
        heights = jax.random.uniform(jax.random.fold_in(jax.random.fold_in(key, 6), dim), (blocks,), jnp.float32, smallest / len(pieces), high / len(pieces))
        return jnp.repeat(jnp.exp(heights), dims[dim] // blocks).reshape((-1,) + (1,) * (len(dims) - dim - 1))

    level = one(*pieces[0])
    for cut in pieces[1:]:
        level = level * one(*cut)
    return level


def scatter_about(own_key, shape, spread, bound, pieces=(), kind=jnp.bfloat16):
    entries = spread * jax.random.normal(own_key, shape, jnp.float32)
    if pieces:
        entries = entries * block_scale(own_key, shape, pieces, -0.22, 0.18)
    return jnp.clip(entries, -bound, bound).astype(kind)


def setup_inputs(seed: int = 0) -> dict:
    key_list = jax.random.split(jax.random.key(seed), 8)
    queries = scatter_about(key_list[0], (HG, NQ, G * DK), 1.0, 6.0, ((1, 4), (2, 2)))
    comp_keys = scatter_about(key_list[1], (KEYS, G * DK), 1.0, 6.0, ((0, 16), (1, 2)))
    comp_values = scatter_about(key_list[2], (KEYS, G * DV), 1.0, 6.0, ((0, 16), (1, 2)))
    outputs = scatter_about(key_list[3], (HG, NQ, G * DV), 0.2, 1.1953125, ((1, 4), (2, 2)))
    grad_out = scatter_about(key_list[4], (HG, NQ, G * DV), 50.0, 300.0, ((1, 4), (2, 2)))
    log_sums = jnp.clip(7.0 + 3.0 * jax.random.uniform(key_list[5], (G, HG, NQ), jnp.float32) ** block_scale(key_list[5], (G, HG, NQ), ((0, 2), (2, 4)), -0.2, 0.2), 7.0, 10.0)
    visible = draw_visible(jax.random.fold_in(key_list[7], 71), 0)
    return dict(queries=queries, comp_keys=comp_keys, comp_values=comp_values, outputs=outputs, grad_out=grad_out, log_sums=log_sums, visible=visible)


def reference(queries, comp_keys, comp_values, outputs, grad_out, log_sums, visible):
    softmax_scale = 1.0 / math.sqrt(DK)
    block_rows = min(512, KEYS)
    blocks = KEYS // block_rows
    query_total = queries.shape[1]
    mask_blocks = visible.reshape(NQB, blocks, block_rows).transpose(1, 0, 2)
    grads_query = []
    grads_key = []
    grads_value = []
    for group_index in range(G):
        query_group = queries[:, :, group_index * DK:(group_index + 1) * DK].astype(jnp.float32)
        grad_group = grad_out[:, :, group_index * DV:(group_index + 1) * DV].astype(jnp.float32)
        out_group = outputs[:, :, group_index * DV:(group_index + 1) * DV].astype(jnp.float32)
        row_delta = lax.optimization_barrier(jnp.sum(grad_group * out_group, axis=2))
        row_lse = log_sums[group_index]
        key_group = comp_keys[:, group_index * DK:(group_index + 1) * DK].reshape(blocks, block_rows, DK)
        value_group = comp_values[:, group_index * DV:(group_index + 1) * DV].reshape(blocks, block_rows, DV)

        def advance(running, inputs, query_group=query_group, grad_group=grad_group, row_delta=row_delta, row_lse=row_lse):
            key_block, value_block, mask_block = inputs
            key_float = key_block.astype(jnp.float32)
            scores = jnp.einsum('hqd,kd->hqk', query_group, key_float) * softmax_scale
            weights = jnp.repeat(mask_block, QBLK, axis=0).astype(jnp.float32)
            probs_full = jnp.exp(scores - row_lse[:, :, None]) * weights[None]
            probs_low = lax.optimization_barrier(probs_full.astype(jnp.bfloat16)).astype(jnp.float32)
            grad_probs = jnp.einsum('hqd,kd->hqk', grad_group, value_block.astype(jnp.float32))
            grad_scores = probs_full * (grad_probs - row_delta[:, :, None])
            grad_low = lax.optimization_barrier(grad_scores.astype(jnp.bfloat16)).astype(jnp.float32)
            value_grad = jnp.einsum('hqk,hqd->kd', probs_low, grad_group)
            key_grad = jnp.einsum('hqk,hqd->kd', grad_low, query_group) * softmax_scale
            query_grad = jnp.einsum('hqk,kd->hqd', grad_low, key_float) * softmax_scale
            return (running + query_grad, (key_grad, value_grad))
        initial = jnp.zeros((HG, query_total, DK), jnp.float32)
        query_sum, (key_parts, value_parts) = lax.scan(advance, initial, (key_group, value_group, mask_blocks))
        grads_query.append(query_sum)
        grads_key.append(key_parts.reshape(KEYS, DK))
        grads_value.append(value_parts.reshape(KEYS, DV))
    return (jnp.concatenate(grads_query, axis=2), jnp.concatenate(grads_key, axis=1), jnp.concatenate(grads_value, axis=1))
```

```python
import functools

import jax
import jax.numpy as jnp
from jax import lax
from jax.experimental import pallas as pl
from jax.experimental.pallas import tpu as pltpu
from jax.sharding import PartitionSpec as P

DK = 192
DV = 128
LANES = 128
HALF = LANES // 2
DIRECT = 9
MESH = pl.DeviceIdType.MESH


def flip(index, bits):
    bit = 1
    while bit <= bits:
        if bits & bit:
            index = index + bit - 2 * bit * ((index // bit) % 2)
        bit *= 2
    return index


def masks(n, parity):
    return [m for m in range(n) if m.bit_count() % 2 == parity]


def low_bit(m):
    return m & -m


def along(m):
    return m ^ ((m >> 1).bit_count() % 2)


def tile_start(group):
    return group * DK // LANES * LANES


def low_lanes(block):
    return lax.broadcasted_iota(jnp.int32, block.shape, block.ndim - 1) < HALF


def half_roll(block):
    return pltpu.roll(block, HALF, block.ndim - 1)


def doubled(first, second, even):
    full = jnp.where(even, first, second)
    half = jnp.where(even, second, first)
    half = jnp.where(low_lanes(half) == even, half, jnp.zeros_like(half))
    return full, half + half_roll(half)


def fold(twice):
    rows = twice.shape[-2] // 2
    top, bottom = twice[..., :rows, :], twice[..., rows:, :]
    return jnp.where(low_lanes(top), top, bottom)


def unfold(folded):
    low = low_lanes(folded)
    turned = half_roll(folded)
    return jnp.concatenate(
        [jnp.where(low, folded, turned), jnp.where(low, turned, folded)], axis=folded.ndim - 2
    )


def dot(a, b, ca, cb):
    return lax.dot_general(a, b, (((ca,), (cb,)), ((), ())), preferred_element_type=jnp.float32)


def kernel(n_pb, n_ka, groups, own_heads, nq, rows, n_blocks, *refs):
    q_hbm, k_hbm, v_hbm, o_hbm, do_hbm, lse_hbm, vis_hbm = refs[:7]
    dq_ref, dk_ref, dv_ref = refs[7:10]
    (
        raw, kv, own, qv, dov, ov, lse, vis, stat, dq_acc, dq_full, dq_s, dq_r, acc, core_r, zs, zr, whole_grad,
        ready, loc_sem, own_s, far_s, ag_s, ag_r, vs_s, vs_r, core_ss, core_rs, z_s, z_r, q_s, q_r,
    ) = refs[10:]

    f32, bf16 = jnp.float32, jnp.bfloat16
    ka = lax.axis_index("ka")
    pb = lax.axis_index("pb")
    scale = DK ** (-0.5)
    heads = own_heads * groups
    group = ka % groups
    even = group % 2 == 0
    first_head = (ka // groups) * heads
    hq = heads * nq
    width = 2 * LANES
    k_start = pl.multiple_of(tile_start(group), LANES)
    v_start = pl.multiple_of(group * DV, LANES)
    head_part = pl.ds(first_head, heads)
    roots = {0: masks(n_pb, 0), 1: masks(n_pb, 1)}
    steps = [along(1 << t) for t in range(n_pb.bit_length() - 1)]
    beside = [1] + roots[0][1:]
    across = [0] + roots[1]

    locals_ = []
    for g in range(groups):
        locals_ += [
            (k_hbm.at[:, pl.ds(tile_start(g), width)], raw.at[g, :, pl.ds(0, width)]),
            (v_hbm.at[:, pl.ds(g * DV, DV)], raw.at[g, :, pl.ds(width, DV)]),
        ]
    locals_ += [(vis_hbm, vis.at[ka])]
    first = len(locals_)
    locals_ += [
        (q_hbm.at[head_part, :, pl.ds(k_start, width)], qv),
        (do_hbm.at[head_part, :, pl.ds(v_start, DV)], dov),
        (o_hbm.at[head_part, :, pl.ds(v_start, DV)], ov),
        (lse_hbm, lse),
    ]
    loc = [pltpu.make_async_copy(a, b, loc_sem.at[i]) for i, (a, b) in enumerate(locals_)]

    barrier = pltpu.get_barrier_semaphore()
    lower = ka * len(across)
    for o in beside:
        peer = flip(pb, o)
        lower = lower + (peer < pb).astype(jnp.int32)

        @pl.when(peer > pb)
        def _(peer=peer):
            pl.semaphore_signal(barrier, inc=1, device_id={"pb": peer}, device_id_type=MESH)

    for z in range(1, n_ka):

        @pl.when(z > ka)
        def _(z=z):
            for o in across:
                pl.semaphore_signal(barrier, inc=1, device_id={"ka": z, "pb": flip(pb, o)}, device_id_type=MESH)

    for c in loc:
        c.start()

    @pl.when(lower > 0)
    def _():
        pl.semaphore_wait(barrier, lower)

    for z in range(n_ka - 1):

        @pl.when(z < ka)
        def _(z=z):
            for o in across:
                pl.semaphore_signal(
                    ready.at[ka, pb], inc=1, device_id={"ka": z, "pb": flip(pb, o)}, device_id_type=MESH
                )

    for o in beside:
        peer = flip(pb, o)

        @pl.when(peer < pb)
        def _(peer=peer):
            pl.semaphore_signal(ready.at[ka, pb], inc=1, device_id={"pb": peer}, device_id_type=MESH)

    def remote(src, dst, s_sem, r_sem, **peer):
        return pltpu.make_async_remote_copy(
            src_ref=src, dst_ref=dst, send_sem=s_sem, recv_sem=r_sem,
            device_id=peer, device_id_type=MESH,
        )

    def other(i):
        return jnp.where(i - 1 >= ka, i, i - 1)

    for c in loc[:first]:
        c.wait()
    for g in range(groups):
        tiles = raw[g]
        full, half = doubled(
            tiles[:, :LANES].astype(f32), tiles[:, LANES:width].astype(f32), jnp.bool_(g % 2 == 0)
        )
        own[g, 0:rows] = tiles[:, width:]
        own[g, rows : 2 * rows] = full.astype(bf16)
        own[g, 2 * rows :] = fold(half).astype(bf16)
    kv[ka, pb] = own[group]

    def is_far(z):
        return (z - ka >= DIRECT) | (ka - z >= DIRECT)

    def send_across(z, later):
        for k, o in enumerate(roots[1]):
            peer = flip(pb, o)
            if later:
                pl.semaphore_wait(ready.at[z, peer], 1)

            def go():
                remote(own.at[z % groups], kv.at[ka, pb], own_s.at[z, k], ag_r.at[ka, pb], ka=z, pb=peer).start()

            if o == 1:
                go()
            else:
                pl.when(is_far(z))(go)
        if later:
            pl.semaphore_wait(ready.at[z, pb], 1)
        remote(vis.at[ka], vis.at[ka], vs_s.at[z], vs_r.at[ka], ka=z).start()

    for z in range(n_ka - 1):

        @pl.when(z < ka)
        def _(z=z):
            send_across(z, False)

    for c in loc[first:]:
        c.wait()
    full, half = doubled(
        qv[:, :, :LANES].astype(f32), qv[:, :, LANES:].astype(f32), even
    )
    qv[:, :, :LANES] = full.astype(bf16)
    qv[:, :, LANES:] = half.astype(bf16)
    product = dov[...].astype(f32) * ov[...].astype(f32)
    stat[1:2, :] = jnp.sum(jnp.transpose(product.reshape(hq, DV)), axis=0, keepdims=True)
    for h in range(heads):
        stat[0:1, h * nq : (h + 1) * nq] = lse[group, pl.ds(first_head + h, 1), :]

    for k, o in enumerate(beside):
        peer = flip(pb, o)

        @pl.when(peer > pb)
        def _(peer=peer):
            pl.semaphore_wait(ready.at[ka, peer], 1)

        if o not in steps:
            continue
        remote(kv.at[ka, pb], kv.at[ka, pb], own_s.at[ka, k], ag_r.at[ka, pb], pb=peer).start()

    for z in range(1, n_ka):

        @pl.when(z > ka)
        def _(z=z):
            send_across(z, True)

    def shard_wait(z, origin):
        remote(kv.at[z, origin], kv.at[z, origin], ag_s.at[z, origin], ag_r.at[z, origin], pb=flip(pb, 1)).wait_recv()

    def place(i):
        return (ka, 0) if i == 0 else (other(i), 1)

    def forward(i, m):
        z, parity = place(i)
        origin = flip(pb, along(m) ^ parity)
        if i or m:
            shard_wait(z, origin)
        bit = n_pb // 2
        while bit > 1:
            if m == 0 or bit < low_bit(m):

                def go(bit=bit):
                    remote(
                        kv.at[z, origin], kv.at[z, origin], far_s.at[i, m + bit], ag_r.at[z, origin],
                        pb=flip(pb, along(bit)),
                    ).start()

                if i:
                    pl.when(jnp.logical_not(is_far(z)))(go)
                elif m:
                    go()
            bit //= 2
        if i or m:
            remote(
                kv.at[z, origin], kv.at[z, origin], ag_s.at[z, origin], ag_r.at[z, origin], pb=flip(pb, 1)
            ).start()

    def relay_a(i):
        if i < n_ka:
            forward(i, 0)

    def relay_b(i):
        if i < n_ka:
            bit = n_pb // 2
            while bit > 1:
                for m in range(bit, n_pb, 2 * bit):
                    forward(i, m)
                bit //= 2

    def arrive(i):
        z, parity = place(i)
        for o in roots[1 - parity]:
            shard_wait(z, flip(pb, o))
        if i:
            remote(vis.at[z], vis.at[z], vs_s.at[z], vs_r.at[z], ka=z).wait_recv()

    per = min(n_pb, max(1, 256 // rows))
    chunk_rows = per * rows

    def compute_chunk(i, z, chunk):
        at = pl.ds(chunk * per, per)
        whole = kv[z, at]
        if per == n_pb:
            seen = vis[z]
        else:
            seen = vis[z, :, pl.ds(pl.multiple_of(chunk * chunk_rows, chunk_rows), chunk_rows)]
        seen = seen.astype(f32)
        block = lax.broadcasted_iota(jnp.int32, (nq, chunk_rows), 0) // (nq // n_blocks)
        mask = jnp.zeros((nq, chunk_rows), f32)
        for b in range(n_blocks):
            mask = jnp.where(block == b, seen[b : b + 1, :], mask)
        mask = jnp.transpose(mask)
        mask = jnp.concatenate([mask] * heads, axis=1)
        values = whole[:, 0:rows].reshape(chunk_rows, DV)
        folded = whole[:, 2 * rows :]
        low = low_lanes(folded)
        nothing = jnp.zeros_like(folded)
        half = jnp.concatenate([jnp.where(low, folded, nothing), jnp.where(low, nothing, folded)], axis=1)
        keys = jnp.concatenate(
            [whole[:, rows : 2 * rows].reshape(chunk_rows, LANES), half.reshape(chunk_rows, LANES)], axis=1
        )
        grad = dov[...].reshape(hq, DV)
        query = qv[...].reshape(hq, width)
        scores = dot(keys, query, 1, 1) * scale
        probs = jnp.exp(scores - stat[0:1, :]) * mask
        grad_probs = dot(values, grad, 1, 1)
        grad_scores = (probs * (grad_probs - stat[1:2, :])).astype(bf16)
        acc[i, at, 0:rows] = dot(probs.astype(bf16), grad, 1, 0).reshape(per, rows, DV)
        key_grad = dot(grad_scores, query, 1, 0)
        acc[i, at, rows : 2 * rows] = key_grad[:, :LANES].reshape(per, rows, LANES)
        acc[i, at, 2 * rows :] = fold(key_grad[:, LANES:].reshape(per, rows, LANES))
        query_grad = dot(grad_scores, keys, 0, 0)
        if i == 0 and per == n_pb:
            dq_acc[...] = query_grad
        else:
            dq_acc[...] += query_grad

    if per < n_pb:
        dq_acc[...] = jnp.zeros_like(dq_acc)

    def compute(i):
        z, parity = place(i)
        if per == n_pb:
            compute_chunk(i, z, 0)
        else:
            lax.fori_loop(0, n_pb // per, lambda c, _: (compute_chunk(i, z, c), 0)[1], 0)
        for k, o in enumerate(roots[1 - parity]):
            remote(
                acc.at[i, flip(pb, o)], core_r.at[i, k], core_ss.at[i, k], core_rs.at[i, k], pb=flip(pb, 1)
            ).start()

    def reduce(i):
        z, parity = place(i)
        for k, o in enumerate(roots[parity]):
            mine = flip(pb, o)
            slot = [m ^ 1 for m in roots[1 - parity]].index(o)
            remote(
                core_r.at[i, slot], core_r.at[i, slot], core_ss.at[i, slot], core_rs.at[i, slot], pb=flip(pb, 1)
            ).wait_recv()
            total = acc[i, mine] + core_r[i, slot]
            if o == 0:
                acc[i, mine] = total
            else:
                zs[i, k] = total.astype(bf16)
                remote(zs.at[i, k], zr.at[ka, k], z_s.at[i, k], z_r.at[ka, k], ka=z, pb=mine).start()

    def send_queries():
        for r in range(1, groups):
            far = flip(ka, r)
            part = dq_acc[pl.ds(pl.multiple_of((far % groups) * own_heads * nq, nq), own_heads * nq), :]
            half = part[:, LANES:]
            half = (half + half_roll(half)).reshape(own_heads, nq, LANES)
            dq_s[r, :, :nq] = part[:, :LANES].reshape(own_heads, nq, LANES).astype(bf16)
            dq_s[r, :, nq:] = fold(half).astype(bf16)
            remote(dq_s.at[r], dq_r.at[r], q_s.at[r], q_r.at[r], ka=far).start()
        mine = dq_acc[pl.ds(pl.multiple_of(group * own_heads * nq, nq), own_heads * nq), :]
        half = mine[:, LANES:]
        dq_full[group, :, :, :LANES] = mine[:, :LANES].reshape(own_heads, nq, LANES)
        dq_full[group, :, :, LANES:] = (half + half_roll(half)).reshape(own_heads, nq, LANES)

    relay_a(1)
    relay_b(0)
    for i in range(n_ka):
        arrive(i)
        relay_a(i + 2)
        relay_b(i + 1)
        compute(i)
        if i == n_ka - 1:
            send_queries()
        if i:
            reduce(i - 1)
    reduce(n_ka - 1)

    def join(pieces, columns):
        tiles = {}
        for g in range(groups):
            full, half = pieces[g]
            at = tile_start(g)
            low = low_lanes(half)
            if g % 2 == 0:
                tiles[at] = full
                tiles[at + LANES] = jnp.where(low, half, 0.0)
            else:
                tiles[at] = jnp.where(low, tiles[at], half) if at in tiles else jnp.where(low, 0.0, half)
                tiles[at + LANES] = full
        return [(at, tile) for at, tile in tiles.items() if at < columns]

    for r in range(1, groups):
        far = flip(ka, r)
        remote(dq_r.at[r], dq_r.at[r], q_s.at[r], q_r.at[r], ka=far).wait_recv()
        got = dq_r[r].astype(f32)
        dq_full[far % groups, :, :, :LANES] = got[:, :nq]
        dq_full[far % groups, :, :, LANES:] = unfold(got[:, nq:])
    pieces = [(dq_full[g, :, :, :LANES], dq_full[g, :, :, LANES:]) for g in range(groups)]
    for at, tile in join(pieces, groups * DK):
        dq_ref[:, :, at : at + LANES] = tile * scale

    zr[ka, 0] = jnp.zeros(zr.shape[2:], bf16)
    for i in range(n_ka):
        z, parity = place(i)
        for k, o in enumerate(roots[parity]):
            if o:
                remote(zr.at[z, k], zr.at[z, k], z_s.at[i, k], z_r.at[z, k], ka=z).wait_recv()
    for g in range(groups):
        total = None
        for z in range(g, n_ka, groups):
            for k in range(n_pb // 2):
                term = zr[z, k].astype(f32)
                total = term if total is None else total + term
        whole_grad[g] = total
    whole_grad[group] += acc[0, pb]
    pieces = []
    for g in range(groups):
        dv_ref[:, g * DV : (g + 1) * DV] = whole_grad[g, 0:rows]
        pieces.append((whole_grad[g, rows : 2 * rows], unfold(whole_grad[g, 2 * rows :])))
    for at, tile in join(pieces, groups * DK):
        dk_ref[:, at : at + LANES] = tile * scale

    for k, o in enumerate(beside):
        if o in steps:
            remote(kv.at[ka, pb], kv.at[ka, pb], own_s.at[ka, k], ag_r.at[ka, pb], pb=flip(pb, 1)).wait_send()
    for i in range(n_ka):
        z, parity = place(i)
        if i:
            for k in range(len(roots[1])):
                remote(own.at[0], kv.at[ka, pb], own_s.at[z, k], ag_r.at[ka, pb], pb=flip(pb, 1)).wait_send() if k == 0 else pl.when(is_far(z))(
                    lambda k=k: remote(own.at[0], kv.at[ka, pb], own_s.at[z, k], ag_r.at[ka, pb], pb=flip(pb, 1)).wait_send())
            remote(vis.at[ka], vis.at[ka], vs_s.at[z], vs_r.at[ka], pb=flip(pb, 1)).wait_send()
        for m in range(0, n_pb, 2):
            bit = n_pb // 2
            while bit > 1:
                if (i or m) and (m == 0 or bit < low_bit(m)):

                    def done(bit=bit, m=m):
                        remote(kv.at[z, pb], kv.at[z, pb], far_s.at[i, m + bit], ag_r.at[z, pb], pb=flip(pb, 1)).wait_send()

                    if i:
                        pl.when(jnp.logical_not(is_far(z)))(done)
                    else:
                        done()
                bit //= 2
        for k, o in enumerate(roots[parity]):
            if o:
                origin = flip(pb, o)
                remote(
                    kv.at[z, origin], kv.at[z, origin], ag_s.at[z, origin], ag_r.at[z, origin], pb=flip(pb, 1)
                ).wait_send()
                remote(zs.at[i, k], zr.at[ka, k], z_s.at[i, k], z_r.at[ka, k], pb=flip(pb, 1)).wait_send()
        for k, o in enumerate(roots[1 - parity]):
            remote(
                acc.at[i, flip(pb, o)], core_r.at[i, k], core_ss.at[i, k], core_rs.at[i, k], pb=flip(pb, 1)
            ).wait_send()
    for r in range(1, groups):
        remote(dq_s.at[r], dq_r.at[r], q_s.at[r], q_r.at[r], pb=flip(pb, 1)).wait_send()


def finish(*refs):
    n = 3
    sem = refs[2 * n]
    copies = [pltpu.make_async_copy(refs[i], refs[n + i], sem.at[i]) for i in range(n)]
    for c in copies:
        c.start()
    for c in copies:
        c.wait()


def per_device(n_pb, n_ka, queries, comp_keys, comp_values, outputs, grad_out, log_sums, visible):
    groups = comp_keys.shape[1] // DK
    all_heads, nq, _ = queries.shape
    heads = all_heads // n_ka
    rows = comp_keys.shape[0]
    n_blocks = visible.shape[0]
    f32, bf16 = jnp.float32, jnp.bfloat16
    width = 2 * LANES
    team = heads * groups
    packed = 2 * rows + rows // 2
    half = n_pb // 2
    dma = pltpu.SemaphoreType.DMA
    scratch = [
        pltpu.VMEM((groups, rows, width + DV), bf16),
        pltpu.VMEM((n_ka, n_pb, packed, LANES), bf16),
        pltpu.VMEM((groups, packed, LANES), bf16),
        pltpu.VMEM((team, nq, width), bf16),
        pltpu.VMEM((team, nq, DV), bf16),
        pltpu.VMEM((team, nq, DV), bf16),
        pltpu.VMEM(log_sums.shape, f32),
        pltpu.VMEM((n_ka,) + visible.shape, jnp.int32),
        pltpu.VMEM((2, team * nq), f32),
        pltpu.VMEM((team * nq, width), f32),
        pltpu.VMEM((groups, heads, nq, width), f32),
        pltpu.VMEM((groups, heads, nq + nq // 2, LANES), bf16),
        pltpu.VMEM((groups, heads, nq + nq // 2, LANES), bf16),
        pltpu.VMEM((n_ka, n_pb, packed, LANES), f32),
        pltpu.VMEM((n_ka, half, packed, LANES), f32),
        pltpu.VMEM((n_ka, half, packed, LANES), bf16),
        pltpu.VMEM((n_ka, half, packed, LANES), bf16),
        pltpu.VMEM((groups, packed, LANES), f32),
        pltpu.SemaphoreType.REGULAR((n_ka, n_pb)),
        dma((5 + 2 * groups,)),
        dma((n_ka, half)),
        dma((n_ka, n_pb)),
        dma((n_ka, n_pb)),
        dma((n_ka, n_pb)),
        dma((n_ka,)),
        dma((n_ka,)),
        dma((n_ka, half)),
        dma((n_ka, half)),
        dma((n_ka, half)),
        dma((n_ka, half)),
        dma((groups,)),
        dma((groups,)),
    ]
    shapes = ((heads, nq, queries.shape[2]), comp_keys.shape, comp_values.shape)
    grads = pl.pallas_call(
        functools.partial(kernel, n_pb, n_ka, groups, heads, nq, rows, n_blocks),
        out_shape=tuple(pltpu.VMEM(s, f32) for s in shapes),
        in_specs=[pl.BlockSpec(memory_space=pl.ANY)] * 7,
        out_specs=[pl.BlockSpec(memory_space=pltpu.VMEM)] * 3,
        scratch_shapes=scratch,
        compiler_params=pltpu.CompilerParams(
            collective_id=0, has_side_effects=True, vmem_limit_bytes=64000 * 1024
        ),
    )(queries, comp_keys, comp_values, outputs, grad_out, log_sums, visible)
    return pl.pallas_call(
        finish,
        out_shape=tuple(jax.ShapeDtypeStruct(s, f32) for s in shapes),
        in_specs=[pl.BlockSpec(memory_space=pltpu.VMEM)] * 3,
        out_specs=[pl.BlockSpec(memory_space=pl.ANY)] * 3,
        scratch_shapes=[dma((3,))],
    )(*[pltpu.with_memory_space_constraint(x, pltpu.VMEM) for x in grads])


def solution(mesh):
    n_pb, n_ka = mesh.shape["pb"], mesh.shape["ka"]
    return jax.shard_map(
        functools.partial(per_device, n_pb, n_ka),
        mesh=mesh,
        in_specs=(
            P(None, "pb", "ga"),
            P(("ka", "pb"), "ga"),
            P(("ka", "pb"), "ga"),
            P(None, "pb", "ga"),
            P(None, "pb", "ga"),
            P("ga", None, "pb"),
            P("pb", "ka"),
        ),
        out_specs=(P("ka", "pb", "ga"), P(("ka", "pb"), "ga"), P(("ka", "pb"), "ga")),
        check_vma=False,
    )
```

```python
import functools

import jax
import jax.numpy as jnp
from jax import lax
from jax.experimental import pallas as pl
from jax.experimental.pallas import tpu as pltpu
from jax.sharding import PartitionSpec as P

DK = 192
DV = 128
LANES = 128
HALF = LANES // 2
MESH = pl.DeviceIdType.MESH


def flip(index, bits):
    bit = 1
    while bit <= bits:
        if bits & bit:
            index = index + bit - 2 * bit * ((index // bit) % 2)
        bit *= 2
    return index


def masks(n, parity):
    return [m for m in range(n) if m.bit_count() % 2 == parity]


def tile_start(group):
    return group * DK // LANES * LANES


def low_lanes(block):
    return lax.broadcasted_iota(jnp.int32, block.shape, block.ndim - 1) < HALF


def half_roll(block):
    return pltpu.roll(block, HALF, block.ndim - 1)


def doubled(first, second, even):
    full = jnp.where(even, first, second)
    half = jnp.where(even, second, first)
    half = jnp.where(low_lanes(half) == even, half, jnp.zeros_like(half))
    return full, half + half_roll(half)


def fold(twice):
    rows = twice.shape[-2] // 2
    top, bottom = twice[..., :rows, :], twice[..., rows:, :]
    return jnp.where(low_lanes(top), top, bottom)


def unfold(folded):
    low = low_lanes(folded)
    turned = half_roll(folded)
    return jnp.concatenate(
        [jnp.where(low, folded, turned), jnp.where(low, turned, folded)], axis=folded.ndim - 2
    )


def batch_size(keys):
    return 1


def dot(a, b, ca, cb):
    return lax.dot_general(a, b, (((ca,), (cb,)), ((), ())), preferred_element_type=jnp.float32)


def kernel(n_pb, n_ka, groups, own_heads, nq, rows, n_blocks, *refs):
    q_hbm, k_hbm, v_hbm, o_hbm, do_hbm, lse_hbm, vis_hbm = refs[:7]
    dq_ref, dk_ref, dv_ref = refs[7:10]
    (
        raw, kv, own, qv, dov, ov, lse, vis, stat, seen_t, dq_acc, dq_full, pair_s, pair_r, dq_s, dq_r, acc, zs, zr,
        whole_grad, ready, loc_sem, own_s, ag_r, vs_s, vs_r, half_s, half_r, z_s, z_r, pair_ss, pair_rs, q_s, q_r,
    ) = refs[10:]

    f32, bf16 = jnp.float32, jnp.bfloat16
    ka = lax.axis_index("ka")
    pb = lax.axis_index("pb")
    mate = flip(pb, 1)
    scale = DK ** (-0.5)
    heads = own_heads * groups
    group = ka % groups
    even = group % 2 == 0
    first_head = (ka // groups) * heads
    part = own_heads * nq
    width = 2 * LANES
    k_start = pl.multiple_of(tile_start(group), LANES)
    v_start = pl.multiple_of(group * DV, LANES)
    roots = {0: masks(n_pb, 0), 1: masks(n_pb, 1)}
    half = n_pb // 2
    beside = [1] + roots[0][1:]
    across = [0] + roots[1]

    locals_ = []
    for g in range(groups):
        locals_ += [
            (k_hbm.at[:, pl.ds(tile_start(g), width)], raw.at[g, :, pl.ds(0, width)]),
            (v_hbm.at[:, pl.ds(g * DV, DV)], raw.at[g, :, pl.ds(width, DV)]),
        ]
    locals_ += [(vis_hbm, vis.at[ka, 0])]
    first = len(locals_)
    for t in range(groups):
        head_part = pl.ds(first_head + flip(group, t) * own_heads, own_heads)
        locals_ += [
            (q_hbm.at[head_part, :, pl.ds(k_start, width)], qv.at[t, 0]),
            (do_hbm.at[head_part, :, pl.ds(v_start, DV)], dov.at[t, 0]),
            (o_hbm.at[head_part, :, pl.ds(v_start, DV)], ov.at[t]),
        ]
    locals_ += [(lse_hbm, lse)]
    loc = [pltpu.make_async_copy(a, b, loc_sem.at[i]) for i, (a, b) in enumerate(locals_)]

    barrier = pltpu.get_barrier_semaphore()
    lower = ka * len(across)
    for o in beside:
        peer = flip(pb, o)
        lower = lower + (peer < pb).astype(jnp.int32)

        @pl.when(peer > pb)
        def _(peer=peer):
            pl.semaphore_signal(barrier, inc=1, device_id={"pb": peer}, device_id_type=MESH)

    for z in range(1, n_ka):

        @pl.when(z > ka)
        def _(z=z):
            for o in across:
                pl.semaphore_signal(barrier, inc=1, device_id={"ka": z, "pb": flip(pb, o)}, device_id_type=MESH)

    for c in loc:
        c.start()

    @pl.when(lower > 0)
    def _():
        pl.semaphore_wait(barrier, lower)

    for z in range(n_ka - 1):

        @pl.when(z < ka)
        def _(z=z):
            for o in across:
                pl.semaphore_signal(
                    ready.at[ka, pb], inc=1, device_id={"ka": z, "pb": flip(pb, o)}, device_id_type=MESH
                )

    for o in beside:
        peer = flip(pb, o)

        @pl.when(peer < pb)
        def _(peer=peer):
            pl.semaphore_signal(ready.at[ka, pb], inc=1, device_id={"pb": peer}, device_id_type=MESH)

    def remote(src, dst, s_sem, r_sem, **peer):
        return pltpu.make_async_remote_copy(
            src_ref=src, dst_ref=dst, send_sem=s_sem, recv_sem=r_sem,
            device_id=peer, device_id_type=MESH,
        )

    for c in loc[:first]:
        c.wait()
    for g in range(groups):
        tiles = raw[g]
        full, twice = doubled(
            tiles[:, :LANES].astype(f32), tiles[:, LANES:width].astype(f32), jnp.bool_(g % 2 == 0)
        )
        own[g, 0:rows] = tiles[:, width:]
        own[g, rows : 2 * rows] = full.astype(bf16)
        own[g, 2 * rows :] = fold(twice).astype(bf16)
    kv[ka, 0] = own[group]

    def shards(z, k, peer):
        return remote(own.at[z % groups], kv.at[ka, k], own_s.at[z, k], ag_r.at[ka, k], ka=z, pb=peer)

    def table(z, s):
        return remote(vis.at[ka, 0], vis.at[ka, s], vs_s.at[z, s], vs_r.at[ka, s], ka=z, pb=flip(pb, s))

    def send_across(z, later):
        for k, o in enumerate(roots[1]):
            peer = flip(pb, o)
            if later:
                pl.semaphore_wait(ready.at[z, peer], 1)
            shards(z, k, peer).start()
            if o == 1:
                table(z, 1).start()
        if later:
            pl.semaphore_wait(ready.at[z, pb], 1)
        table(z, 0).start()

    for z in range(n_ka - 1):

        @pl.when(z < ka)
        def _(z=z):
            send_across(z, False)

    def to_mate(n, src, dst):
        return remote(src, dst, half_s.at[n], half_r.at[n], pb=mate)

    halves = []
    for t in range(groups):
        halves += [to_mate(2 * t, qv.at[t, 0], qv.at[t, 1]), to_mate(2 * t + 1, dov.at[t, 0], dov.at[t, 1])]
    halves += [to_mate(2 * groups, stat.at[0], stat.at[1])]

    @pl.when(mate > pb)
    def _():
        pl.semaphore_wait(ready.at[ka, mate], 1)

    table_mate = remote(vis.at[ka, 0], vis.at[ka, 1], vs_s.at[ka, 1], vs_r.at[ka, 1], pb=mate)
    table_mate.start()
    for c in loc[first:]:
        c.wait()
    for t in range(groups):
        halves[2 * t + 1].start()
        full, twice = doubled(qv[t, 0, :, :, :LANES].astype(f32), qv[t, 0, :, :, LANES:].astype(f32), even)
        qv[t, 0, :, :, :LANES] = full.astype(bf16)
        qv[t, 0, :, :, LANES:] = twice.astype(bf16)
        halves[2 * t].start()
    for t in range(groups):
        product = dov[t, 0].astype(f32) * ov[t].astype(f32)
        product = jnp.sum(jnp.transpose(product.reshape(part, DV)), axis=0, keepdims=True)
        stat[0, 1:2, t * part : (t + 1) * part] = product
        for h in range(own_heads):
            at = t * part + h * nq
            head = first_head + flip(group, t) * own_heads + h
            stat[0, 0:1, at : at + nq] = lse[group, pl.ds(head, 1), :]
    halves[-1].start()

    for k, o in enumerate(roots[0]):
        if o:
            peer = flip(pb, o)

            @pl.when(peer > pb)
            def _(peer=peer):
                pl.semaphore_wait(ready.at[ka, peer], 1)

            shards(ka, k, peer).start()

    for z in range(1, n_ka):

        @pl.when(z > ka)
        def _(z=z):
            send_across(z, True)

    def place(i):
        return (ka, 0) if i == 0 else (jnp.where(ka >= i, i - 1, i), 1)

    per = min(half, max(1, 256 // rows))
    chunk_rows = per * rows

    def compute_chunk(members, origins, chunk):
        at = pl.ds(chunk * per, per)
        count = len(members) * per
        whole = jnp.concatenate([kv[z, at] for _, z in members], axis=0)
        values = whole[:, 0:rows].reshape(count * rows, DV)
        folded = whole[:, 2 * rows :]
        low = low_lanes(folded)
        nothing = jnp.zeros_like(folded)
        pieces = jnp.concatenate([jnp.where(low, folded, nothing), jnp.where(low, nothing, folded)], axis=1)
        keys = jnp.concatenate(
            [whole[:, rows : 2 * rows].reshape(count * rows, LANES), pieces.reshape(count * rows, LANES)], axis=1
        )
        sides = []
        block = lax.broadcasted_iota(jnp.int32, (count * rows, nq), 1) // (nq // n_blocks)
        for s in range(2):
            flags = jnp.concatenate(
                [
                    seen_t[n, s, pl.ds(pl.multiple_of(o * rows, rows), rows), :]
                    for n, some in enumerate(origins)
                    for o in some
                ],
                axis=0,
            )
            mask = jnp.zeros((count * rows, nq), f32)
            for b in range(n_blocks):
                mask = jnp.where(block == b, flags[:, b : b + 1], mask)
            sides += [mask] * own_heads
        mask = jnp.concatenate(sides, axis=1)
        first_round, last_round = members[0][0] == 0, members[-1][0] == n_ka - 1
        value_grad = key_grad = None
        for t in reversed(range(groups)):
            seg = slice(t * part, (t + 1) * part)
            lse_row, delta_row = [
                jnp.concatenate([stat[0, n : n + 1, seg], stat[1, n : n + 1, seg]], axis=1) for n in range(2)
            ]
            grad = dov[t].reshape(2 * part, DV)
            query = qv[t].reshape(2 * part, width)
            probs = jnp.exp(dot(keys, query, 1, 1) * scale - lse_row) * mask
            grad_probs = dot(values, grad, 1, 1)
            grad_scores = (probs * (grad_probs - delta_row)).astype(bf16)
            query_grad = dot(grad_scores, keys, 0, 0)
            if first_round and per == half:
                dq_acc[t] = query_grad.reshape(2, part, width)
            else:
                dq_acc[t] += query_grad.reshape(2, part, width)
            if last_round and t and per == half:
                send_pair(t)
            more = dot(probs.astype(bf16), grad, 1, 0), dot(grad_scores, query, 1, 0)
            value_grad = more[0] if value_grad is None else value_grad + more[0]
            key_grad = more[1] if key_grad is None else key_grad + more[1]
        value_grad = value_grad.reshape(count, rows, DV)
        key_grad = key_grad.reshape(count, rows, width)
        folded = fold(key_grad[:, :, LANES:])
        for n, (i, _) in enumerate(members):
            some = slice(n * per, (n + 1) * per)
            acc[i, at, 0:rows] = value_grad[some]
            acc[i, at, rows : 2 * rows] = key_grad[some, :, :LANES]
            acc[i, at, 2 * rows :] = folded[some]

    if per < half:
        dq_acc[...] = jnp.zeros_like(dq_acc)

    def pair_copy(t):
        return remote(pair_s.at[t], pair_r.at[t], pair_ss.at[t], pair_rs.at[t], pb=mate)

    def twice_half(x):
        right = x[:, LANES:]
        return x[:, :LANES].reshape(own_heads, nq, LANES), (right + half_roll(right)).reshape(own_heads, nq, LANES)

    def send_pair(t):
        full, twice = twice_half(dq_acc[t, 1])
        pair_s[t, :, :nq] = full.astype(bf16)
        pair_s[t, :, nq:] = fold(twice).astype(bf16)
        pair_copy(t).start()

    def compute(batch):
        members = [(i, place(i)[0]) for i in batch]
        for n, (i, z) in enumerate(members):
            for k, o in enumerate(roots[place(i)[1]]):
                if i or o:
                    remote(own.at[0], kv.at[z, k], own_s.at[z, k], ag_r.at[z, k], pb=mate).wait_recv()
            for s in range(2):
                if i or s:
                    remote(vis.at[z, s], vis.at[z, s], vs_s.at[z, s], vs_r.at[z, s], pb=mate).wait_recv()
                flags = vis[z, s].astype(f32)
                flags = jnp.concatenate([flags, jnp.zeros((LANES - n_blocks, flags.shape[1]), f32)], axis=0)
                seen_t[n, s] = jnp.transpose(flags)
        if per == half:
            compute_chunk(members, [[flip(pb, o) for o in roots[place(i)[1]]] for i in batch], 0)
        else:

            def step(c, _):
                origins = []
                for i in batch:
                    some = []
                    for n in range(per):
                        k = c * per + n
                        o = sum(jnp.where(k == m, mask, 0) for m, mask in enumerate(roots[place(i)[1]]))
                        origin, bit = 0, 1
                        while bit < n_pb:
                            origin = origin + bit * (((o // bit) % 2 + (pb // bit) % 2) % 2)
                            bit *= 2
                        some.append(origin)
                    origins.append(some)
                compute_chunk(members, origins, c)
                return 0

            lax.fori_loop(0, half // per, step, 0)
        for i, z in members:
            for k, o in enumerate(roots[place(i)[1]]):
                if i or o:
                    zs[i, k] = acc[i, k].astype(bf16)
                    remote(zs.at[i, k], zr.at[ka, k], z_s.at[i, k], z_r.at[ka, k], ka=z, pb=flip(pb, o)).start()

    for n, c in enumerate(halves):
        c.wait_recv()
    rounds = batch_size(half * rows)
    for i in range(0, n_ka, rounds):
        compute(range(i, min(i + rounds, n_ka)))
    for t in reversed(range(groups)):
        if t == 0 or per < half:
            send_pair(t)

    def paired(t):
        pair_copy(t).wait_recv()
        full, twice = twice_half(dq_acc[t, 0])
        got = pair_r[t].astype(f32)
        return full + got[:, :nq], twice + unfold(got[:, nq:])

    def query_copy(t):
        return remote(dq_s.at[t], dq_r.at[t], q_s.at[t], q_r.at[t], ka=flip(ka, t))

    for t in range(1, groups):
        full, twice = paired(t)
        dq_s[t, :, :nq] = full.astype(bf16)
        dq_s[t, :, nq:] = fold(twice).astype(bf16)
        query_copy(t).start()
    full, twice = paired(0)
    dq_full[group, :, :, :LANES] = full
    dq_full[group, :, :, LANES:] = twice

    def join(pieces, columns):
        tiles = {}
        for g in range(groups):
            full, half = pieces[g]
            at = tile_start(g)
            low = low_lanes(half)
            if g % 2 == 0:
                tiles[at] = full
                tiles[at + LANES] = jnp.where(low, half, 0.0)
            else:
                tiles[at] = jnp.where(low, tiles[at], half) if at in tiles else jnp.where(low, 0.0, half)
                tiles[at + LANES] = full
        return [(at, tile) for at, tile in tiles.items() if at < columns]

    zr[ka, 0] = jnp.zeros(zr.shape[2:], bf16)
    for i in range(n_ka):
        z, parity = place(i)
        for k, o in enumerate(roots[parity]):
            if i or o:
                remote(zr.at[z, k], zr.at[z, k], z_s.at[i, k], z_r.at[z, k], ka=z).wait_recv()
    for g in range(groups):
        total = None
        for z in range(g, n_ka, groups):
            for k in range(half):
                term = zr[z, k].astype(f32)
                total = term if total is None else total + term
        whole_grad[g] = total
    whole_grad[group] += acc[0, 0]
    pieces = []
    for g in range(groups):
        dv_ref[:, g * DV : (g + 1) * DV] = whole_grad[g, 0:rows]
        pieces.append((whole_grad[g, rows : 2 * rows], unfold(whole_grad[g, 2 * rows :])))
    for at, tile in join(pieces, groups * DK):
        dk_ref[:, at : at + LANES] = tile * scale

    for t in range(1, groups):
        query_copy(t).wait_recv()
        got = dq_r[t].astype(f32)
        dq_full[flip(group, t), :, :, :LANES] = got[:, :nq]
        dq_full[flip(group, t), :, :, LANES:] = unfold(got[:, nq:])
    pieces = [(dq_full[g, :, :, :LANES], dq_full[g, :, :, LANES:]) for g in range(groups)]
    for at, tile in join(pieces, groups * DK):
        dq_ref[:, :, at : at + LANES] = tile * scale

    for c in halves:
        c.wait_send()
    table_mate.wait_send()
    for i in range(n_ka):
        z, parity = place(i)
        for k, o in enumerate(roots[parity]):
            if i or o:
                shards(z, k, mate).wait_send()
                remote(zs.at[i, k], zr.at[ka, k], z_s.at[i, k], z_r.at[ka, k], pb=mate).wait_send()
        if i:
            for s in range(2):
                remote(vis.at[ka, 0], vis.at[ka, s], vs_s.at[z, s], vs_r.at[ka, s], pb=mate).wait_send()
    for t in range(groups):
        pair_copy(t).wait_send()
        if t:
            remote(dq_s.at[t], dq_r.at[t], q_s.at[t], q_r.at[t], pb=mate).wait_send()


def finish(*refs):
    n = 3
    sem = refs[2 * n]
    copies = [pltpu.make_async_copy(refs[i], refs[n + i], sem.at[i]) for i in range(n)]
    for c in copies:
        c.start()
    for c in copies:
        c.wait()


def per_device(n_pb, n_ka, queries, comp_keys, comp_values, outputs, grad_out, log_sums, visible):
    groups = comp_keys.shape[1] // DK
    all_heads, nq, _ = queries.shape
    heads = all_heads // n_ka
    rows = comp_keys.shape[0]
    n_blocks = visible.shape[0]
    f32, bf16 = jnp.float32, jnp.bfloat16
    width = 2 * LANES
    team = heads * groups
    packed = 2 * rows + rows // 2
    half = n_pb // 2
    dma = pltpu.SemaphoreType.DMA
    strip = nq + nq // 2
    scratch = [
        pltpu.VMEM((groups, rows, width + DV), bf16),
        pltpu.VMEM((n_ka, half, packed, LANES), bf16),
        pltpu.VMEM((groups, packed, LANES), bf16),
        pltpu.VMEM((groups, 2, heads, nq, width), bf16),
        pltpu.VMEM((groups, 2, heads, nq, DV), bf16),
        pltpu.VMEM((groups, heads, nq, DV), bf16),
        pltpu.VMEM(log_sums.shape, f32),
        pltpu.VMEM((n_ka, 2) + visible.shape, jnp.int32),
        pltpu.VMEM((2, 2, team * nq), f32),
        pltpu.VMEM((batch_size(half * rows), 2, n_pb * rows, LANES), f32),
        pltpu.VMEM((groups, 2, heads * nq, width), f32),
        pltpu.VMEM((groups, heads, nq, width), f32),
        pltpu.VMEM((groups, heads, strip, LANES), bf16),
        pltpu.VMEM((groups, heads, strip, LANES), bf16),
        pltpu.VMEM((groups, heads, strip, LANES), bf16),
        pltpu.VMEM((groups, heads, strip, LANES), bf16),
        pltpu.VMEM((n_ka, half, packed, LANES), f32),
        pltpu.VMEM((n_ka, half, packed, LANES), bf16),
        pltpu.VMEM((n_ka, half, packed, LANES), bf16),
        pltpu.VMEM((groups, packed, LANES), f32),
        pltpu.SemaphoreType.REGULAR((n_ka, n_pb)),
        dma((6 + 5 * groups,)),
        dma((n_ka, half)),
        dma((n_ka, half)),
        dma((n_ka, 2)),
        dma((n_ka, 2)),
        dma((2 * groups + 1,)),
        dma((2 * groups + 1,)),
        dma((n_ka, half)),
        dma((n_ka, half)),
        dma((groups,)),
        dma((groups,)),
        dma((groups,)),
        dma((groups,)),
    ]
    shapes = ((heads, nq, queries.shape[2]), comp_keys.shape, comp_values.shape)
    grads = pl.pallas_call(
        functools.partial(kernel, n_pb, n_ka, groups, heads, nq, rows, n_blocks),
        out_shape=tuple(pltpu.VMEM(s, f32) for s in shapes),
        in_specs=[pl.BlockSpec(memory_space=pl.ANY)] * 7,
        out_specs=[pl.BlockSpec(memory_space=pltpu.VMEM)] * 3,
        scratch_shapes=scratch,
        compiler_params=pltpu.CompilerParams(
            collective_id=0, has_side_effects=True, vmem_limit_bytes=64000 * 1024
        ),
    )(queries, comp_keys, comp_values, outputs, grad_out, log_sums, visible)
    return pl.pallas_call(
        finish,
        out_shape=tuple(jax.ShapeDtypeStruct(s, f32) for s in shapes),
        in_specs=[pl.BlockSpec(memory_space=pltpu.VMEM)] * 3,
        out_specs=[pl.BlockSpec(memory_space=pl.ANY)] * 3,
        scratch_shapes=[dma((3,))],
    )(*[pltpu.with_memory_space_constraint(x, pltpu.VMEM) for x in grads])


def solution(mesh):
    n_pb, n_ka = mesh.shape["pb"], mesh.shape["ka"]
    return jax.shard_map(
        functools.partial(per_device, n_pb, n_ka),
        mesh=mesh,
        in_specs=(
            P(None, "pb", "ga"),
            P(("ka", "pb"), "ga"),
            P(("ka", "pb"), "ga"),
            P(None, "pb", "ga"),
            P(None, "pb", "ga"),
            P("ga", None, "pb"),
            P("pb", "ka"),
        ),
        out_specs=(P("ka", "pb", "ga"), P(("ka", "pb"), "ga"), P(("ka", "pb"), "ga")),
        check_vma=False,
    )
```

```python
import functools

import jax
import jax.numpy as jnp
from jax import lax
from jax.experimental import pallas as pl
from jax.experimental.pallas import tpu as pltpu
from jax.sharding import PartitionSpec as P

DK = 192
DV = 128
LANES = 128
HALF = LANES // 2
MESH = pl.DeviceIdType.MESH


def flip(index, bits):
    bit = 1
    while bit <= bits:
        if bits & bit:
            index = index + bit - 2 * bit * ((index // bit) % 2)
        bit *= 2
    return index


def masks(n, parity):
    return [m for m in range(n) if m.bit_count() % 2 == parity]


def tile_start(group):
    return group * DK // LANES * LANES


def low_lanes(block):
    return lax.broadcasted_iota(jnp.int32, block.shape, block.ndim - 1) < HALF


def half_roll(block):
    return pltpu.roll(block, HALF, block.ndim - 1)


def doubled(first, second, even):
    full = jnp.where(even, first, second)
    half = jnp.where(even, second, first)
    half = jnp.where(low_lanes(half) == even, half, jnp.zeros_like(half))
    return full, half + half_roll(half)


def fold(twice):
    rows = twice.shape[-2] // 2
    top, bottom = twice[..., :rows, :], twice[..., rows:, :]
    return jnp.where(low_lanes(top), top, bottom)


def unfold(folded):
    low = low_lanes(folded)
    turned = half_roll(folded)
    return jnp.concatenate(
        [jnp.where(low, folded, turned), jnp.where(low, turned, folded)], axis=folded.ndim - 2
    )


def batch_size(keys):
    return 1


def dot(a, b, ca, cb):
    return lax.dot_general(a, b, (((ca,), (cb,)), ((), ())), preferred_element_type=jnp.float32)


def kernel(n_pb, n_ka, groups, own_heads, nq, rows, n_blocks, *refs):
    q_hbm, k_hbm, v_hbm, o_hbm, do_hbm, lse_hbm, vis_hbm = refs[:7]
    dq_ref, dk_ref, dv_ref = refs[7:10]
    (
        raw, kv, own, qv, dov, ov, lse, vis, stat, seen_t, dq_acc, dq_full, pair_s, pair_r, dq_s, dq_r, acc, zs, zr,
        whole_grad, ready, loc_sem, own_s, ag_r, vs_s, vs_r, half_s, half_r, z_s, z_r, pair_ss, pair_rs, q_s, q_r,
    ) = refs[10:]

    f32, bf16 = jnp.float32, jnp.bfloat16
    ka = lax.axis_index("ka")
    pb = lax.axis_index("pb")
    mate = flip(pb, 1)
    scale = DK ** (-0.5)
    heads = own_heads * groups
    group = ka % groups
    even = group % 2 == 0
    first_head = (ka // groups) * heads
    part = own_heads * nq
    width = 2 * LANES
    k_start = pl.multiple_of(tile_start(group), LANES)
    v_start = pl.multiple_of(group * DV, LANES)
    roots = {0: masks(n_pb, 0), 1: masks(n_pb, 1)}
    half = n_pb // 2
    beside = [1] + roots[0][1:]
    across = [0] + roots[1]

    locals_ = []
    for g in range(groups):
        locals_ += [
            (k_hbm.at[:, pl.ds(tile_start(g), width)], raw.at[g, :, pl.ds(0, width)]),
            (v_hbm.at[:, pl.ds(g * DV, DV)], raw.at[g, :, pl.ds(width, DV)]),
        ]
    locals_ += [(vis_hbm, vis.at[ka, 0])]
    first = len(locals_)
    for t in range(groups):
        head_part = pl.ds(first_head + flip(group, t) * own_heads, own_heads)
        locals_ += [
            (q_hbm.at[head_part, :, pl.ds(k_start, width)], qv.at[t, 0]),
            (do_hbm.at[head_part, :, pl.ds(v_start, DV)], dov.at[t, 0]),
            (o_hbm.at[head_part, :, pl.ds(v_start, DV)], ov.at[t]),
        ]
    locals_ += [(lse_hbm, lse)]
    loc = [pltpu.make_async_copy(a, b, loc_sem.at[i]) for i, (a, b) in enumerate(locals_)]

    barrier = pltpu.get_barrier_semaphore()
    lower = ka * len(across)
    for o in beside:
        peer = flip(pb, o)
        lower = lower + (peer < pb).astype(jnp.int32)

        @pl.when(peer > pb)
        def _(peer=peer):
            pl.semaphore_signal(barrier, inc=1, device_id={"pb": peer}, device_id_type=MESH)

    for z in range(1, n_ka):

        @pl.when(z > ka)
        def _(z=z):
            for o in across:
                pl.semaphore_signal(barrier, inc=1, device_id={"ka": z, "pb": flip(pb, o)}, device_id_type=MESH)

    for c in loc:
        c.start()

    @pl.when(lower > 0)
    def _():
        pl.semaphore_wait(barrier, lower)

    for z in range(n_ka - 1):

        @pl.when(z < ka)
        def _(z=z):
            for o in across:
                pl.semaphore_signal(
                    ready.at[ka, pb], inc=1, device_id={"ka": z, "pb": flip(pb, o)}, device_id_type=MESH
                )

    for o in beside:
        peer = flip(pb, o)

        @pl.when(peer < pb)
        def _(peer=peer):
            pl.semaphore_signal(ready.at[ka, pb], inc=1, device_id={"pb": peer}, device_id_type=MESH)

    def remote(src, dst, s_sem, r_sem, **peer):
        return pltpu.make_async_remote_copy(
            src_ref=src, dst_ref=dst, send_sem=s_sem, recv_sem=r_sem,
            device_id=peer, device_id_type=MESH,
        )

    for c in loc[:first]:
        c.wait()
    for g in range(groups):
        tiles = raw[g]
        full, twice = doubled(
            tiles[:, :LANES].astype(f32), tiles[:, LANES:width].astype(f32), jnp.bool_(g % 2 == 0)
        )
        own[g, 0:rows] = tiles[:, width:]
        own[g, rows : 2 * rows] = full.astype(bf16)
        own[g, 2 * rows :] = fold(twice).astype(bf16)
    kv[ka, 0] = own[group]

    def shards(z, k, peer):
        return remote(own.at[z % groups], kv.at[ka, k], own_s.at[z, k], ag_r.at[ka, k], ka=z, pb=peer)

    def table(z, s):
        return remote(vis.at[ka, 0], vis.at[ka, s], vs_s.at[z, s], vs_r.at[ka, s], ka=z, pb=flip(pb, s))

    def send_across(z, later):
        for k, o in enumerate(roots[1]):
            peer = flip(pb, o)
            if later:
                pl.semaphore_wait(ready.at[z, peer], 1)
            shards(z, k, peer).start()
            if o == 1:
                table(z, 1).start()
        if later:
            pl.semaphore_wait(ready.at[z, pb], 1)
        table(z, 0).start()

    for z in [n ^ 1 for n in range(n_ka)]:

        @pl.when(z < ka)
        def _(z=z):
            send_across(z, False)

    def to_mate(n, src, dst):
        return remote(src, dst, half_s.at[n], half_r.at[n], pb=mate)

    halves = []
    for t in range(groups):
        halves += [to_mate(2 * t, qv.at[t, 0], qv.at[t, 1]), to_mate(2 * t + 1, dov.at[t, 0], dov.at[t, 1])]
    halves += [to_mate(2 * groups, stat.at[0], stat.at[1])]

    @pl.when(mate > pb)
    def _():
        pl.semaphore_wait(ready.at[ka, mate], 1)

    table_mate = remote(vis.at[ka, 0], vis.at[ka, 1], vs_s.at[ka, 1], vs_r.at[ka, 1], pb=mate)
    table_mate.start()
    for c in loc[first:]:
        c.wait()
    for t in range(groups):
        halves[2 * t + 1].start()
        full, twice = doubled(qv[t, 0, :, :, :LANES].astype(f32), qv[t, 0, :, :, LANES:].astype(f32), even)
        qv[t, 0, :, :, :LANES] = full.astype(bf16)
        qv[t, 0, :, :, LANES:] = twice.astype(bf16)
        halves[2 * t].start()
    for t in range(groups):
        product = dov[t, 0].astype(f32) * ov[t].astype(f32)
        product = jnp.sum(jnp.transpose(product.reshape(part, DV)), axis=0, keepdims=True)
        stat[0, 1:2, t * part : (t + 1) * part] = product
        for h in range(own_heads):
            at = t * part + h * nq
            head = first_head + flip(group, t) * own_heads + h
            stat[0, 0:1, at : at + nq] = lse[group, pl.ds(head, 1), :]
    halves[-1].start()

    for k, o in enumerate(roots[0]):
        if o:
            peer = flip(pb, o)

            @pl.when(peer > pb)
            def _(peer=peer):
                pl.semaphore_wait(ready.at[ka, peer], 1)

            shards(ka, k, peer).start()

    for z in range(1, n_ka):

        @pl.when(z > ka)
        def _(z=z):
            send_across(z, True)

    def place(i):
        return (ka, 0) if i == 0 else (jnp.where(ka >= i, i - 1, i), 1)

    per = min(half, max(1, 256 // rows))
    chunk_rows = per * rows

    def compute_chunk(members, origins, chunk):
        at = pl.ds(chunk * per, per)
        count = len(members) * per
        whole = jnp.concatenate([kv[z, at] for _, z in members], axis=0)
        values = whole[:, 0:rows].reshape(count * rows, DV)
        folded = whole[:, 2 * rows :]
        low = low_lanes(folded)
        nothing = jnp.zeros_like(folded)
        pieces = jnp.concatenate([jnp.where(low, folded, nothing), jnp.where(low, nothing, folded)], axis=1)
        keys = jnp.concatenate(
            [whole[:, rows : 2 * rows].reshape(count * rows, LANES), pieces.reshape(count * rows, LANES)], axis=1
        )
        sides = []
        block = lax.broadcasted_iota(jnp.int32, (count * rows, nq), 1) // (nq // n_blocks)
        for s in range(2):
            flags = jnp.concatenate(
                [
                    seen_t[n, s, pl.ds(pl.multiple_of(o * rows, rows), rows), :]
                    for n, some in enumerate(origins)
                    for o in some
                ],
                axis=0,
            )
            mask = jnp.zeros((count * rows, nq), f32)
            for b in range(n_blocks):
                mask = jnp.where(block == b, flags[:, b : b + 1], mask)
            sides += [mask] * own_heads
        mask = jnp.concatenate(sides, axis=1)
        first_round, last_round = members[0][0] == 0, members[-1][0] == n_ka - 1
        value_grad = key_grad = None
        for t in reversed(range(groups)):
            seg = slice(t * part, (t + 1) * part)
            lse_row, delta_row = [
                jnp.concatenate([stat[0, n : n + 1, seg], stat[1, n : n + 1, seg]], axis=1) for n in range(2)
            ]
            grad = dov[t].reshape(2 * part, DV)
            query = qv[t].reshape(2 * part, width)
            probs = jnp.exp(dot(keys, query, 1, 1) * scale - lse_row) * mask
            grad_probs = dot(values, grad, 1, 1)
            grad_scores = (probs * (grad_probs - delta_row)).astype(bf16)
            query_grad = dot(grad_scores, keys, 0, 0)
            if first_round and per == half:
                dq_acc[t] = query_grad.reshape(2, part, width)
            else:
                dq_acc[t] += query_grad.reshape(2, part, width)
            more = dot(probs.astype(bf16), grad, 1, 0), dot(grad_scores, query, 1, 0)
            value_grad = more[0] if value_grad is None else value_grad + more[0]
            key_grad = more[1] if key_grad is None else key_grad + more[1]
        value_grad = value_grad.reshape(count, rows, DV)
        key_grad = key_grad.reshape(count, rows, width)
        folded = fold(key_grad[:, :, LANES:])
        for n, (i, _) in enumerate(members):
            some = slice(n * per, (n + 1) * per)
            acc[i, at, 0:rows] = value_grad[some]
            acc[i, at, rows : 2 * rows] = key_grad[some, :, :LANES]
            acc[i, at, 2 * rows :] = folded[some]

    if per < half:
        dq_acc[...] = jnp.zeros_like(dq_acc)

    def pair_copy(t):
        return remote(pair_s.at[t], pair_r.at[t], pair_ss.at[t], pair_rs.at[t], pb=mate)

    def twice_half(x):
        right = x[:, LANES:]
        return x[:, :LANES].reshape(own_heads, nq, LANES), (right + half_roll(right)).reshape(own_heads, nq, LANES)

    def send_pair(t):
        full, twice = twice_half(dq_acc[t, 1])
        pair_s[t, :, :nq] = full.astype(bf16)
        pair_s[t, :, nq:] = fold(twice).astype(bf16)
        pair_copy(t).start()

    def compute(batch):
        members = [(i, place(i)[0]) for i in batch]
        for n, (i, z) in enumerate(members):
            for k, o in enumerate(roots[place(i)[1]]):
                if i or o:
                    remote(own.at[0], kv.at[z, k], own_s.at[z, k], ag_r.at[z, k], pb=mate).wait_recv()
            for s in range(2):
                if i or s:
                    remote(vis.at[z, s], vis.at[z, s], vs_s.at[z, s], vs_r.at[z, s], pb=mate).wait_recv()
                flags = vis[z, s].astype(f32)
                flags = jnp.concatenate([flags, jnp.zeros((LANES - n_blocks, flags.shape[1]), f32)], axis=0)
                seen_t[n, s] = jnp.transpose(flags)
        if per == half:
            compute_chunk(members, [[flip(pb, o) for o in roots[place(i)[1]]] for i in batch], 0)
        else:

            def step(c, _):
                origins = []
                for i in batch:
                    some = []
                    for n in range(per):
                        k = c * per + n
                        o = sum(jnp.where(k == m, mask, 0) for m, mask in enumerate(roots[place(i)[1]]))
                        origin, bit = 0, 1
                        while bit < n_pb:
                            origin = origin + bit * (((o // bit) % 2 + (pb // bit) % 2) % 2)
                            bit *= 2
                        some.append(origin)
                    origins.append(some)
                compute_chunk(members, origins, c)
                return 0

            lax.fori_loop(0, half // per, step, 0)
        for i, z in members:
            for k, o in enumerate(roots[place(i)[1]]):
                if i or o:
                    zs[i, k] = acc[i, k].astype(bf16)
                    remote(zs.at[i, k], zr.at[ka, k], z_s.at[i, k], z_r.at[ka, k], ka=z, pb=flip(pb, o)).start()

    for n, c in enumerate(halves):
        c.wait_recv()
    rounds = batch_size(half * rows)
    for i in range(0, n_ka, rounds):
        compute(range(i, min(i + rounds, n_ka)))
    for t in reversed(range(groups)):
        send_pair(t)

    def paired(t):
        pair_copy(t).wait_recv()
        full, twice = twice_half(dq_acc[t, 0])
        got = pair_r[t].astype(f32)
        return full + got[:, :nq], twice + unfold(got[:, nq:])

    def query_copy(t):
        return remote(dq_s.at[t], dq_r.at[t], q_s.at[t], q_r.at[t], ka=flip(ka, t))

    for t in range(1, groups):
        full, twice = paired(t)
        dq_s[t, :, :nq] = full.astype(bf16)
        dq_s[t, :, nq:] = fold(twice).astype(bf16)
        query_copy(t).start()
    full, twice = paired(0)
    dq_full[group, :, :, :LANES] = full
    dq_full[group, :, :, LANES:] = twice

    def join(pieces, columns):
        tiles = {}
        for g in range(groups):
            full, half = pieces[g]
            at = tile_start(g)
            low = low_lanes(half)
            if g % 2 == 0:
                tiles[at] = full
                tiles[at + LANES] = jnp.where(low, half, 0.0)
            else:
                tiles[at] = jnp.where(low, tiles[at], half) if at in tiles else jnp.where(low, 0.0, half)
                tiles[at + LANES] = full
        return [(at, tile) for at, tile in tiles.items() if at < columns]

    zr[ka, 0] = jnp.zeros(zr.shape[2:], bf16)
    for i in range(n_ka):
        z, parity = place(i)
        for k, o in enumerate(roots[parity]):
            if i or o:
                remote(zr.at[z, k], zr.at[z, k], z_s.at[i, k], z_r.at[z, k], ka=z).wait_recv()
    for g in range(groups):
        total = None
        for z in range(g, n_ka, groups):
            for k in range(half):
                term = zr[z, k].astype(f32)
                total = term if total is None else total + term
        whole_grad[g] = total
    whole_grad[group] += acc[0, 0]
    pieces = []
    for g in range(groups):
        dv_ref[:, g * DV : (g + 1) * DV] = whole_grad[g, 0:rows]
        pieces.append((whole_grad[g, rows : 2 * rows], unfold(whole_grad[g, 2 * rows :])))
    for at, tile in join(pieces, groups * DK):
        dk_ref[:, at : at + LANES] = tile * scale

    for t in range(1, groups):
        query_copy(t).wait_recv()
        got = dq_r[t].astype(f32)
        dq_full[flip(group, t), :, :, :LANES] = got[:, :nq]
        dq_full[flip(group, t), :, :, LANES:] = unfold(got[:, nq:])
    pieces = [(dq_full[g, :, :, :LANES], dq_full[g, :, :, LANES:]) for g in range(groups)]
    for at, tile in join(pieces, groups * DK):
        dq_ref[:, :, at : at + LANES] = tile * scale

    for c in halves:
        c.wait_send()
    table_mate.wait_send()
    for i in range(n_ka):
        z, parity = place(i)
        for k, o in enumerate(roots[parity]):
            if i or o:
                shards(z, k, mate).wait_send()
                remote(zs.at[i, k], zr.at[ka, k], z_s.at[i, k], z_r.at[ka, k], pb=mate).wait_send()
        if i:
            for s in range(2):
                remote(vis.at[ka, 0], vis.at[ka, s], vs_s.at[z, s], vs_r.at[ka, s], pb=mate).wait_send()
    for t in range(groups):
        pair_copy(t).wait_send()
        if t:
            remote(dq_s.at[t], dq_r.at[t], q_s.at[t], q_r.at[t], pb=mate).wait_send()


def finish(*refs):
    n = 3
    sem = refs[2 * n]
    copies = [pltpu.make_async_copy(refs[i], refs[n + i], sem.at[i]) for i in range(n)]
    for c in copies:
        c.start()
    for c in copies:
        c.wait()


def per_device(n_pb, n_ka, queries, comp_keys, comp_values, outputs, grad_out, log_sums, visible):
    groups = comp_keys.shape[1] // DK
    all_heads, nq, _ = queries.shape
    heads = all_heads // n_ka
    rows = comp_keys.shape[0]
    n_blocks = visible.shape[0]
    f32, bf16 = jnp.float32, jnp.bfloat16
    width = 2 * LANES
    team = heads * groups
    packed = 2 * rows + rows // 2
    half = n_pb // 2
    dma = pltpu.SemaphoreType.DMA
    strip = nq + nq // 2
    scratch = [
        pltpu.VMEM((groups, rows, width + DV), bf16),
        pltpu.VMEM((n_ka, half, packed, LANES), bf16),
        pltpu.VMEM((groups, packed, LANES), bf16),
        pltpu.VMEM((groups, 2, heads, nq, width), bf16),
        pltpu.VMEM((groups, 2, heads, nq, DV), bf16),
        pltpu.VMEM((groups, heads, nq, DV), bf16),
        pltpu.VMEM(log_sums.shape, f32),
        pltpu.VMEM((n_ka, 2) + visible.shape, jnp.int32),
        pltpu.VMEM((2, 2, team * nq), f32),
        pltpu.VMEM((batch_size(half * rows), 2, n_pb * rows, LANES), f32),
        pltpu.VMEM((groups, 2, heads * nq, width), f32),
        pltpu.VMEM((groups, heads, nq, width), f32),
        pltpu.VMEM((groups, heads, strip, LANES), bf16),
        pltpu.VMEM((groups, heads, strip, LANES), bf16),
        pltpu.VMEM((groups, heads, strip, LANES), bf16),
        pltpu.VMEM((groups, heads, strip, LANES), bf16),
        pltpu.VMEM((n_ka, half, packed, LANES), f32),
        pltpu.VMEM((n_ka, half, packed, LANES), bf16),
        pltpu.VMEM((n_ka, half, packed, LANES), bf16),
        pltpu.VMEM((groups, packed, LANES), f32),
        pltpu.SemaphoreType.REGULAR((n_ka, n_pb)),
        dma((6 + 5 * groups,)),
        dma((n_ka, half)),
        dma((n_ka, half)),
        dma((n_ka, 2)),
        dma((n_ka, 2)),
        dma((2 * groups + 1,)),
        dma((2 * groups + 1,)),
        dma((n_ka, half)),
        dma((n_ka, half)),
        dma((groups,)),
        dma((groups,)),
        dma((groups,)),
        dma((groups,)),
    ]
    shapes = ((heads, nq, queries.shape[2]), comp_keys.shape, comp_values.shape)
    grads = pl.pallas_call(
        functools.partial(kernel, n_pb, n_ka, groups, heads, nq, rows, n_blocks),
        out_shape=tuple(pltpu.VMEM(s, f32) for s in shapes),
        in_specs=[pl.BlockSpec(memory_space=pl.ANY)] * 7,
        out_specs=[pl.BlockSpec(memory_space=pltpu.VMEM)] * 3,
        scratch_shapes=scratch,
        compiler_params=pltpu.CompilerParams(
            collective_id=0, has_side_effects=True, vmem_limit_bytes=64000 * 1024
        ),
    )(queries, comp_keys, comp_values, outputs, grad_out, log_sums, visible)
    return pl.pallas_call(
        finish,
        out_shape=tuple(jax.ShapeDtypeStruct(s, f32) for s in shapes),
        in_specs=[pl.BlockSpec(memory_space=pltpu.VMEM)] * 3,
        out_specs=[pl.BlockSpec(memory_space=pl.ANY)] * 3,
        scratch_shapes=[dma((3,))],
    )(*[pltpu.with_memory_space_constraint(x, pltpu.VMEM) for x in grads])


def solution(mesh):
    n_pb, n_ka = mesh.shape["pb"], mesh.shape["ka"]
    return jax.shard_map(
        functools.partial(per_device, n_pb, n_ka),
        mesh=mesh,
        in_specs=(
            P(None, "pb", "ga"),
            P(("ka", "pb"), "ga"),
            P(("ka", "pb"), "ga"),
            P(None, "pb", "ga"),
            P(None, "pb", "ga"),
            P("ga", None, "pb"),
            P("pb", "ka"),
        ),
        out_specs=(P("ka", "pb", "ga"), P(("ka", "pb"), "ga"), P(("ka", "pb"), "ga")),
        check_vma=False,
    )
```
